32 devices in a mesh: dom: 32 (over z, y, x, core).
Axes of the slice: x: 2, y: 2, z: 4, core: 2. Of those that a mesh axis runs over, the one named last changes fastest.
Arguments:
- positions: float32 [3, 131072], P(None, 'dom'), may hold values from -1.5 to 1.5
- velocity: float32 [3, 131072], P(None, 'dom'), may hold values from -6 to 6
- density_weight: float32 [131072], P('dom'), may hold values from 0.5 to 2
- embed_strength: float32 [131072], P('dom'), may hold values from 0.5 to 2
- occupied: int32 [131072], P('dom'), may hold values 0 or 1
- send_list: int32 [32, 8, 8], P('dom'), may hold values from 0 to 31, as said below
- send_count: int32 [32, 8], P('dom'), may hold values from 0 to 8, as said below
- pair_tiles: int32 [1024, 24], P('dom'), may hold values from 0 to 95, as said below
- pair_count: int32 [1024], P('dom'), may hold values from 1 to 24, as said below
- migrate_dest: int32 [1024], P('dom'), may hold values from 0 to 31, as said below
Outputs:
- force: float32 [3, 131072], P(None, 'dom')
- energy: float32 [131072], P('dom')
- moved: float32 [7, 262144], P(None, 'dom')
- moved_count: int32 [32], P('dom')
The draws below stay inside these ranges and needn't reach their ends.
Inputs may be any that keep to these rules, and one draw needn't show every extreme that they name: `send_list`: for one domain and one offset the entries are distinct local tile indices. send_count[s, k] counts the tiles domain s sends to domain s - o_k; it is 0 where that domain does not exist and 8 for some pairs. `pair_tiles`: entries index the frame of the tile's domain; a tile's entries are distinct and its first entry is its own local index. `pair_count`: the first tile of every domain uses all 24 slots. `migrate_dest`: A tile's new domain is within 4 of its domain; at most 4 tiles go from one domain to any other, at most 64 tiles to one domain, and both bounds are reached in every draw.
All inputs are finite; a program needn't handle non-finite values. No bound on the sum of `occupied` on one device may be relied on, other than what follows from the above.
Results may differ from the reference program's by a relative error of at most 0.0003.
Values sent between devices are 32-bit elements; how exact they have to be, the bound alone decides.
A program may use at most 64 MiB of HBM per device.

```python
import math
import jax
import jax.numpy as jnp
from jax import lax

TILE = 128
TILES_DEV = 32
PAIRS = 24
GMAX = 8
RADIUS = 4
MMAX = 4
SPAN = 8
CAP = 64
DOMAINS = 32
TILES = 1024
ATOMS = 131072


def offset_list_drawn():
    return [position - RADIUS for position in range(RADIUS)] + [position + 1 for position in range(RADIUS)]


def draw_send_list(key, part):
    keys = jax.random.split(key, DOMAINS * SPAN)
    chosen = jax.vmap(lambda single: jax.random.permutation(single, TILES_DEV)[:GMAX])(keys)
    return chosen.reshape(DOMAINS, SPAN, GMAX).astype(jnp.int32)


def draw_send_count(key, part):
    offsets = jnp.array(offset_list_drawn(), dtype=jnp.int32)
    counts = jax.random.randint(jax.random.fold_in(key, 11), (DOMAINS, SPAN), 0, GMAX + 1).astype(jnp.int32)
    source = jnp.arange(DOMAINS, dtype=jnp.int32)[:, None]
    offset_ids = jnp.arange(SPAN, dtype=jnp.int32)[None, :]
    target = source - offsets[None, :]
    counts = jnp.where((source + offset_ids) % SPAN == 0, GMAX, counts)
    counts = jnp.where((target >= 0) & (target < DOMAINS), counts, 0)
    return counts.astype(jnp.int32)


def draw_pair_tiles(key, part):
    frame_size = TILES_DEV + SPAN * GMAX
    scores = jax.random.randint(jax.random.fold_in(key, 21), (TILES, frame_size), 0, 1 << 20).astype(jnp.int32)
    column = jnp.arange(frame_size, dtype=jnp.int32)[None, :]
    scores = scores * frame_size + column
    own_local = (jnp.arange(TILES, dtype=jnp.int32) % TILES_DEV)[:, None]
    scores = jnp.where(column == own_local, (1 << 20) * frame_size + frame_size, scores)
    chosen = jax.lax.top_k(scores, PAIRS)[1]
    return chosen.astype(jnp.int32)


def draw_pair_count(key, part):
    counts = jax.random.randint(jax.random.fold_in(key, 31), (TILES,), 1, PAIRS + 1).astype(jnp.int32)
    first = jnp.arange(TILES, dtype=jnp.int32) % TILES_DEV == 0
    return jnp.where(first, PAIRS, counts).astype(jnp.int32)


def draw_migrate_dest(key, part):
    offsets = jnp.array(offset_list_drawn(), dtype=jnp.int32)
    hottest = jax.random.randint(jax.random.fold_in(key, 41), (), RADIUS, DOMAINS - RADIUS).astype(jnp.int32)
    counts = jax.random.randint(jax.random.fold_in(key, 42), (DOMAINS, SPAN), 0, MMAX + 1).astype(jnp.int32)
    source = jnp.arange(DOMAINS, dtype=jnp.int32)[:, None]
    target = source + offsets[None, :]
    counts = jnp.where((target >= 0) & (target < DOMAINS), counts, 0)
    counts = jnp.where(target == hottest, MMAX, counts)
    counts = jnp.where(source == hottest, 0, counts)
    keys = jax.random.split(jax.random.fold_in(key, 43), DOMAINS)
    orders = jax.vmap(lambda single: jax.random.permutation(single, TILES_DEV))(keys).astype(jnp.int32)
    rank_of = jnp.argsort(orders, axis=1, stable=True).astype(jnp.int32)
    limits = jnp.cumsum(counts, axis=1).astype(jnp.int32)
    which = jnp.sum((rank_of[:, :, None] >= limits[:, None, :]).astype(jnp.int32), axis=2)
    strides = jnp.concatenate([offsets, jnp.zeros((1,), jnp.int32)])
    return (source + strides[which]).reshape(TILES).astype(jnp.int32)


def with_ends(values, stream_key, low, largest):
    index_at = [jax.random.randint(jax.random.fold_in(stream_key, axis), (), 0, length) for axis, length in enumerate(values.shape)]
    longest = values.shape.index(max(values.shape))
    beside = index_at[:longest] + [(index_at[longest] + 1) % values.shape[longest]] + index_at[longest + 1:]
    return values.at[tuple(index_at)].set(low).at[tuple(beside)].set(largest)


def shard_levels(key, shape, shards, smallest, high):
    def one(dim, blocks):
        steps = jax.random.uniform(jax.random.fold_in(jax.random.fold_in(key, 6), dim), (blocks,), jnp.float32, smallest / len(shards), high / len(shards))
        return jnp.repeat(jnp.exp(steps), shape[dim] // blocks).reshape((-1,) + (1,) * (len(shape) - dim - 1))

    factor_of = one(*shards[0])
    for cut in shards[1:]:
        factor_of = factor_of * one(*cut)
    return factor_of


def normal_values(rng, shape, spread, most, cuts=(), kind=jnp.bfloat16):
    loudness = shard_levels(rng, shape, cuts, -0.22, 0.18) if cuts else 1.0
    values = jax.random.normal(rng, shape, jnp.float32) * spread * loudness
    return jnp.minimum(jnp.maximum(values, -most), most).astype(kind)


def setup_inputs(seed: int = 0) -> dict:
    key_list = jax.random.split(jax.random.key(seed), 11)
    return {
        "positions": jnp.clip(jax.random.uniform(key_list[0], (3, ATOMS), jnp.float32, -1.5, 1.5) * shard_levels(key_list[0], (3, ATOMS), ((1, 32),), -0.4, 0.0), -1.5, 1.5),
        "velocity": normal_values(key_list[1], (3, ATOMS), 1.0, 6.0, ((1, 32),), jnp.float32),
        "density_weight": jnp.clip(jnp.exp(math.log(2.0) - 1.3862944 * jax.random.uniform(key_list[2], (ATOMS,), jnp.float32) ** shard_levels(key_list[2], (ATOMS,), ((0, 32),), -0.2, 0.2)), 0.5, 2.0),
        "embed_strength": jnp.clip(jnp.exp(math.log(2.0) - 1.3862944 * jax.random.uniform(key_list[3], (ATOMS,), jnp.float32) ** shard_levels(key_list[3], (ATOMS,), ((0, 32),), -0.2, 0.2)), 0.5, 2.0),
        "occupied": with_ends((jax.random.randint(key_list[4], (ATOMS,), 0, 4) < 3).astype(jnp.int32), jax.random.fold_in(key_list[4], 1), 0, 1),
        "send_list": draw_send_list(jax.random.fold_in(key_list[10], 71), 0),
        "send_count": draw_send_count(jax.random.fold_in(key_list[10], 71), 0),
        "pair_tiles": draw_pair_tiles(jax.random.fold_in(key_list[10], 71), 0),
        "pair_count": draw_pair_count(jax.random.fold_in(key_list[10], 71), 0),
        "migrate_dest": draw_migrate_dest(jax.random.fold_in(key_list[10], 71), 0),
    }


CUTOFF_SQUARE = 4.0
REPULSE = 0.05
TIME_STEP = 0.05
EXACT_PRODUCT = lax.Precision.HIGHEST

def offset_list():
    return [position - RADIUS for position in range(RADIUS)] + [position + 1 for position in range(RADIUS)]

def pair_weights(own_occ, near_occ, slot_list, used_count, tile_ids):
    tile_width = own_occ.shape[-1]
    used_mask = (jnp.arange(slot_list.shape[1], dtype=jnp.int32)[None, :] < used_count[:, None]).astype(jnp.float32)
    itself = (slot_list == tile_ids[:, None]).astype(jnp.float32)
    identity_mask = jnp.eye(tile_width, dtype=jnp.float32)
    weight = used_mask[:, :, None, None] * own_occ[:, None, :, None] * near_occ[:, :, None, :]
    return weight * (1.0 - itself[:, :, None, None] * identity_mask[None, None])

def closeness(own_pos, near_pos):
    distance = jnp.zeros(near_pos.shape[:2] + (own_pos.shape[2], near_pos.shape[3]), jnp.float32)
    for coordinate in range(3):
        difference = own_pos[:, None, coordinate, :, None] - near_pos[:, :, coordinate, None, :]
        distance = distance + difference * difference
    return jnp.maximum(1.0 - distance / CUTOFF_SQUARE, 0.0)

def density_terms(own_pos, own_occ, near_pos, near_chi, near_occ, slot_list, used_count, tile_ids):
    weight = pair_weights(own_occ, near_occ, slot_list, used_count, tile_ids)
    within = closeness(own_pos, near_pos)
    reach_cube = weight * within * within * within
    density = lax.optimization_barrier(jnp.sum(reach_cube * near_chi[:, :, None, :], axis=(1, 3)))
    pair_energy = lax.optimization_barrier(jnp.sum(reach_cube * within, axis=(1, 3)))
    return (density, pair_energy)

def force_terms(own_pos, own_occ, own_chi, own_slope, near_pos, near_chi, near_occ, near_slope, slot_list, used_count, tile_ids):
    weight = pair_weights(own_occ, near_occ, slot_list, used_count, tile_ids)
    within = closeness(own_pos, near_pos)
    square = within * within
    mixed_slope = own_slope[:, None, :, None] * near_chi[:, :, None, :] + near_slope[:, :, None, :] * own_chi[:, None, :, None]
    pair_coef = weight * (2.0 / CUTOFF_SQUARE) * (3.0 * square * mixed_slope + 4.0 * REPULSE * square * within)
    total_coef = lax.optimization_barrier(jnp.sum(pair_coef, axis=(1, 3)))
    pulled = jnp.einsum('bpij,bpcj->bci', pair_coef, near_pos, precision=EXACT_PRODUCT)
    return own_pos * total_coef[:, None, :] - pulled

def ghost_tiles(per_domain, send_list, send_count):
    domains = per_domain.shape[0]
    offsets = jnp.array(offset_list(), dtype=jnp.int32)
    source = jnp.arange(domains, dtype=jnp.int32)[:, None] + offsets[None, :]
    inside = (source >= 0) & (source < domains)
    clipped = jnp.clip(source, 0, domains - 1).astype(jnp.int32)
    offset_ids = jnp.arange(SPAN, dtype=jnp.int32)[None, :]
    tile_list = send_list[clipped, offset_ids]
    counts = send_count[clipped, offset_ids]
    live_mask = inside[:, :, None] & (jnp.arange(GMAX, dtype=jnp.int32)[None, None, :] < counts[:, :, None])
    picked = per_domain[clipped[:, :, None], tile_list]
    live_float = live_mask.astype(jnp.float32).reshape(live_mask.shape + (1,) * (picked.ndim - 3))
    return (picked * live_float).reshape((domains, SPAN * GMAX) + per_domain.shape[2:])

def reference(positions, velocity, density_weight, embed_strength, occupied, send_list, send_count, pair_tiles, pair_count, migrate_dest):
    domains = send_list.shape[0]
    tiles_here = pair_tiles.shape[0] // domains
    tile_width = TILE
    filled = occupied.astype(jnp.float32).reshape(domains, tiles_here, tile_width)
    pos_tiles = positions.reshape(3, domains, tiles_here, tile_width).transpose(1, 2, 0, 3)
    vel_tiles = velocity.reshape(3, domains, tiles_here, tile_width).transpose(1, 2, 0, 3)
    weight_tiles = density_weight.reshape(domains, tiles_here, tile_width)
    embed_tiles = embed_strength.reshape(domains, tiles_here, tile_width)
    packed = jnp.concatenate([pos_tiles, weight_tiles[:, :, None], filled[:, :, None]], axis=2)
    frame_tiles = jnp.concatenate([packed, ghost_tiles(packed, send_list, send_count)], axis=1)
    slot_tiles = pair_tiles.reshape(domains, tiles_here, PAIRS)
    used_tiles = pair_count.reshape(domains, tiles_here)
    tile_ids = jnp.arange(tiles_here, dtype=jnp.int32)

    def density_domain(batch_items):
        native, frames, slot_list, used_count = batch_items
        nearby = frames[slot_list]
        return density_terms(native[:, 0:3], native[:, 4], nearby[:, :, 0:3], nearby[:, :, 3], nearby[:, :, 4], slot_list, used_count, tile_ids)
    density, pair_energy = lax.map(density_domain, (packed, frame_tiles, slot_tiles, used_tiles))
    root_term = jnp.sqrt(1.0 + density)
    slope_tiles = -0.5 * embed_tiles * filled / root_term
    energy_tiles = filled * (-embed_tiles * root_term + 0.5 * REPULSE * pair_energy)
    slope_frame = jnp.concatenate([slope_tiles, ghost_tiles(slope_tiles, send_list, send_count)], axis=1)

    def force_domain(batch_items):
        native, frames, slot_list, used_count, own_slope, frame_slope = batch_items
        nearby = frames[slot_list]
        near_slope = frame_slope[slot_list]
        return force_terms(native[:, 0:3], native[:, 4], native[:, 3], own_slope, nearby[:, :, 0:3], nearby[:, :, 3], nearby[:, :, 4], near_slope, slot_list, used_count, tile_ids)
    force_tiles = lax.map(force_domain, (packed, frame_tiles, slot_tiles, used_tiles, slope_tiles, slope_frame))
    new_vel = vel_tiles + TIME_STEP * force_tiles
    new_pos = pos_tiles + TIME_STEP * new_vel
    payload = jnp.concatenate([new_pos, new_vel, filled[:, :, None]], axis=2).reshape(domains * tiles_here, 7, tile_width)
    onehot = (migrate_dest[:, None] == jnp.arange(domains, dtype=jnp.int32)[None, :]).astype(jnp.int32)
    before = (jnp.cumsum(onehot, axis=0) - onehot).astype(jnp.int32)
    slot_index = lax.optimization_barrier(jnp.sum(onehot * before, axis=1)).astype(jnp.int32)
    moved_tiles = jnp.zeros((domains * CAP, 7, tile_width), jnp.float32).at[migrate_dest * CAP + slot_index].set(payload)
    tile_atoms = lax.optimization_barrier(jnp.sum(occupied.reshape(domains * tiles_here, tile_width), axis=1)).astype(jnp.int32)
    moved_count = lax.optimization_barrier(jnp.sum(onehot * tile_atoms[:, None], axis=0)).astype(jnp.int32)
    force = force_tiles.transpose(2, 0, 1, 3).reshape(3, domains * tiles_here * tile_width)
    energy = energy_tiles.reshape(domains * tiles_here * tile_width)
    moved = moved_tiles.transpose(1, 0, 2).reshape(7, domains * CAP * tile_width)
    return (force, energy, moved, moved_count)
```

```python
import functools

import jax
import jax.numpy as jnp
from jax import lax
from jax.experimental import pallas as pl
from jax.experimental.pallas import tpu as pltpu
from jax.sharding import PartitionSpec as P

TILE = 128
RADIUS = 4
MMAX = 4
REPULSE = 0.05
TIME_STEP = 0.05
FAR = 1e15
MESH = pl.DeviceIdType.MESH
OFFSETS = [position - RADIUS for position in range(RADIUS)] + [
    position + 1 for position in range(RADIUS)
]
VMEM = pl.BlockSpec(memory_space=pltpu.VMEM)
SMEM = pl.BlockSpec(memory_space=pltpu.SMEM)
ANY = pl.BlockSpec(memory_space=pl.ANY)
WIDE = 60 * 1024 * 1024


def exists(device, domains):
    return jnp.logical_and(device >= 0, device < domains)


def greet(me, domains):
    barrier = pltpu.get_barrier_semaphore()
    for offset in OFFSETS:

        @pl.when(exists(me + offset, domains))
        def _():
            pl.semaphore_signal(
                barrier, inc=1, device_id=(me + offset,), device_id_type=MESH
            )

    peers = jnp.minimum(me, RADIUS) + jnp.minimum(domains - 1 - me, RADIUS)
    pl.semaphore_wait(barrier, peers)


def frame_kernel(
    domains,
    send_list,
    send_count,
    positions,
    density,
    occupied,
    dest,
    own,
    ghost,
    dests,
    outbox,
    dest_row,
    send_sem,
    recv_sem,
    dest_send,
    dest_recv,
):
    me = lax.axis_index("dom")
    tiles = own.shape[0]
    ghosts = send_list.shape[2]
    filled = occupied[...].astype(jnp.float32)
    weight = density[...] * filled
    own[...] = jnp.zeros_like(own)
    for t in range(tiles):
        here = filled[t : t + 1, :]
        for c in range(3):
            own[t, c : c + 1, :] = jnp.where(
                here > 0, 0.5 * positions[c : c + 1, t * TILE : (t + 1) * TILE], FAR
            )
        own[t, 3:4, :] = weight[t : t + 1, :]
        own[t, 4:5, :] = here
    dest_row[...] = jnp.full_like(dest_row, -1)
    dest_row[:, 0:tiles] = dest[...]
    row = lax.broadcasted_iota(jnp.int32, (8, TILE), 0)
    empty = jnp.where(row < 3, FAR, 0.0)
    for k in range(len(OFFSETS)):
        used = send_count[0, k]
        for g in range(ghosts):
            outbox[k, g] = jnp.where(g < used, own[send_list[0, k, g]], empty)
    greet(me, domains)
    for k, offset in enumerate(OFFSETS):

        @pl.when(exists(me - offset, domains))
        def _():
            pltpu.make_async_remote_copy(
                src_ref=outbox.at[k],
                dst_ref=ghost.at[k],
                send_sem=send_sem.at[k],
                recv_sem=recv_sem.at[k],
                device_id=(me - offset,),
                device_id_type=MESH,
            ).start()
            pltpu.make_async_remote_copy(
                src_ref=dest_row,
                dst_ref=dests.at[k],
                send_sem=dest_send.at[k],
                recv_sem=dest_recv.at[k],
                device_id=(me - offset,),
                device_id_type=MESH,
            ).start()

        @pl.when(jnp.logical_not(exists(me + offset, domains)))
        def _():
            for g in range(ghosts):
                ghost[k, g] = empty
            dests[k] = jnp.full(dests.shape[1:], -1, jnp.int32)

    for k, offset in enumerate(OFFSETS):

        @pl.when(exists(me - offset, domains))
        def _():
            pltpu.make_async_copy(outbox.at[k], outbox.at[k], send_sem.at[k]).wait()
            pltpu.make_async_copy(dest_row, dest_row, dest_send.at[k]).wait()

        @pl.when(exists(me + offset, domains))
        def _():
            pltpu.make_async_copy(ghost.at[k], ghost.at[k], recv_sem.at[k]).wait()
            pltpu.make_async_copy(dests.at[k], dests.at[k], dest_recv.at[k]).wait()


def exchange_kernel(domains, sign, outbox, inbox, send_sem, recv_sem):
    me = lax.axis_index("dom")
    greet(me, domains)
    for k, offset in enumerate(OFFSETS):

        @pl.when(exists(me + sign * offset, domains))
        def _():
            pltpu.make_async_remote_copy(
                src_ref=outbox.at[k],
                dst_ref=inbox.at[k],
                send_sem=send_sem.at[k],
                recv_sem=recv_sem.at[k],
                device_id=(me + sign * offset,),
                device_id_type=MESH,
            ).start()

    for k, offset in enumerate(OFFSETS):

        @pl.when(exists(me + sign * offset, domains))
        def _():
            pltpu.make_async_copy(outbox.at[k], outbox.at[k], send_sem.at[k]).wait()

        @pl.when(exists(me - sign * offset, domains))
        def _():
            pltpu.make_async_copy(inbox.at[k], inbox.at[k], recv_sem.at[k]).wait()


def exchange(blocks, domains, sign, collective_id):
    count = len(OFFSETS)
    return pl.pallas_call(
        functools.partial(exchange_kernel, domains, sign),
        out_shape=jax.ShapeDtypeStruct(blocks.shape, blocks.dtype),
        in_specs=[VMEM],
        out_specs=VMEM,
        scratch_shapes=[
            pltpu.SemaphoreType.DMA((count,)),
            pltpu.SemaphoreType.DMA((count,)),
        ],
        compiler_params=pltpu.CompilerParams(
            collective_id=collective_id, has_side_effects=True
        ),
        name=f"exchange_{collective_id}",
    )(blocks)


def spread(source, first, count, wide, rows):
    group = TILE // 8

    def step(b, carry):
        block = source[pl.ds(b * group, group)].reshape(TILE, TILE).T
        for f in range(group):
            for n, c in enumerate(rows):
                lane = f * 8 + c
                wide[first + b * group + f, n] = jnp.broadcast_to(
                    block[:, lane : lane + 1], (TILE, TILE)
                )
        return carry

    lax.fori_loop(0, count // group, step, 0)


def density_kernel(
    pair_tiles, pair_count, send_list, own, ghost, embed, energy, slope, outbox, wide
):
    tiles, frame_ghosts = own.shape[0], ghost.shape[0]
    spread(own, 0, tiles, wide, (0, 1, 2, 3))
    spread(ghost, tiles, frame_ghosts, wide, (0, 1, 2, 3))

    def tile_step(t, carry):
        mine = own[t]
        x, y, z = [jnp.broadcast_to(mine[c : c + 1], (8, TILE)) for c in range(3)]

        def pair_step(p, sums):
            rho, pair = sums
            near = pair_tiles[t, p]
            for j in range(TILE // 8):
                rows = pl.ds(j * 8, 8)
                dx = x - wide[near, 0, rows]
                dy = y - wide[near, 1, rows]
                dz = z - wide[near, 2, rows]
                reach = jnp.maximum(1.0 - (dx * dx + dy * dy + dz * dz), 0.0)
                square = reach * reach
                rho = rho + square * reach * wide[near, 3, rows]
                pair = pair + square * square
            return rho, pair

        zero = jnp.zeros((8, TILE), jnp.float32)
        rho, pair = lax.fori_loop(0, pair_count[t], pair_step, (zero, zero))
        weight, filled = mine[3:4], mine[4:5]
        rho = jnp.sum(rho, axis=0, keepdims=True) - weight
        pair = jnp.sum(pair, axis=0, keepdims=True) - filled
        root = jnp.sqrt(1.0 + rho)
        strength = embed[pl.ds(t, 1), :]
        slope[pl.ds(t, 1), :] = -0.5 * strength * filled / root
        energy[pl.ds(t, 1), :] = filled * (-strength * root + 0.5 * REPULSE * pair)
        return carry

    lax.fori_loop(0, tiles, tile_step, 0)
    for k in range(send_list.shape[1]):
        for g in range(send_list.shape[2]):
            outbox[k, g : g + 1, :] = slope[pl.ds(send_list[0, k, g], 1), :]


def force_kernel(
    domains,
    pair_tiles,
    pair_count,
    dest,
    own,
    ghost,
    slope,
    ghost_slope,
    positions,
    velocity,
    force,
    outbox,
    stay,
    wide,
    packed,
    ranks,
):
    me = lax.axis_index("dom")
    tiles, frame_ghosts = own.shape[0], ghost.shape[0]
    spans = len(OFFSETS)
    each = frame_ghosts // spans
    packed[0:tiles] = own[...]
    packed[tiles:] = ghost[...]
    for t in range(tiles):
        packed[t, 5:6, :] = 3.0 * slope[t : t + 1, :]
    for k, offset in enumerate(OFFSETS):
        real = exists(me + offset, domains)
        for g in range(each):
            packed[tiles + k * each + g, 5:6, :] = jnp.where(
                real, 3.0 * ghost_slope[k, g : g + 1, :], 0.0
            )
    spread(packed, 0, tiles + frame_ghosts, wide, (0, 1, 2, 3, 5))
    for k in range(spans + 1):
        ranks[k] = 0

    def tile_step(t, carry):
        mine = packed[t]
        x, y, z, weight, tilt = [
            jnp.broadcast_to(mine[c : c + 1], (8, TILE)) for c in (0, 1, 2, 3, 5)
        ]

        def pair_step(p, sums):
            fx, fy, fz = sums
            near = pair_tiles[t, p]
            for j in range(TILE // 8):
                rows = pl.ds(j * 8, 8)
                dx = x - wide[near, 0, rows]
                dy = y - wide[near, 1, rows]
                dz = z - wide[near, 2, rows]
                reach = jnp.maximum(1.0 - (dx * dx + dy * dy + dz * dz), 0.0)
                mixed = tilt * wide[near, 3, rows] + weight * wide[near, 4, rows]
                coef = reach * reach * (mixed + (4.0 * REPULSE) * reach)
                fx = fx + coef * dx
                fy = fy + coef * dy
                fz = fz + coef * dz
            return fx, fy, fz

        zero = jnp.zeros((8, TILE), jnp.float32)
        sums = lax.fori_loop(0, pair_count[t], pair_step, (zero, zero, zero))
        filled = mine[4:5]
        columns = pl.ds(pl.multiple_of(t * TILE, TILE), TILE)
        pull = filled * jnp.concatenate(
            [jnp.sum(s, axis=0, keepdims=True) for s in sums], axis=0
        )
        force[:, columns] = pull
        new_vel = velocity[:, columns] + TIME_STEP * pull
        new_pos = positions[:, columns] + TIME_STEP * new_vel
        tile = jnp.concatenate([new_pos, new_vel, filled, jnp.zeros_like(filled)], axis=0)
        relative = dest[t] - me
        place = jnp.where(relative < 0, relative + RADIUS, relative + RADIUS - 1)
        place = jnp.where(relative == 0, spans, place)
        rank = ranks[place]
        ranks[place] = rank + 1

        @pl.when(relative == 0)
        def _():
            stay[rank] = tile

        @pl.when(relative != 0)
        def _():
            outbox[place, rank] = tile

        return carry

    lax.fori_loop(0, tiles, tile_step, 0)


def settle_kernel(dest, dests, inbox, stay, moved, count):
    me = lax.axis_index("dom")
    tiles, slots = dest.shape[0], moved.shape[1] // TILE
    rows = moved.shape[0]
    spans = len(OFFSETS)

    def put(e, tile, atoms):
        moved[:, pl.ds(pl.multiple_of(e * TILE, TILE), TILE)] = tile[0:rows]
        return atoms + tile

    def hits(value_of):
        total = jnp.int32(0)
        for i in range(tiles):
            total = total + (value_of(i) == me).astype(jnp.int32)
        return total

    slot = jnp.int32(0)
    atoms = jnp.zeros((8, TILE), jnp.float32)

    for k in range(spans):
        if k == RADIUS:
            here = hits(lambda i: dest[i])
            atoms = lax.fori_loop(
                0, here, lambda r, a, s=slot: put(s + r, stay[r], a), atoms
            )
            slot = slot + here
        here = hits(lambda i: dests[k, 0, i])
        atoms = lax.fori_loop(
            0, here, lambda r, a, s=slot: put(s + r, inbox[spans - 1 - k, r], a), atoms
        )
        slot = slot + here

    def clear(e, carry):
        moved[:, pl.ds(pl.multiple_of(e * TILE, TILE), TILE)] = jnp.zeros(
            (rows, TILE), jnp.float32
        )
        return carry

    lax.fori_loop(slot, slots, clear, 0)
    count[0] = jnp.sum(atoms[6:7]).astype(jnp.int32)


def per_device(
    positions,
    velocity,
    density_weight,
    embed_strength,
    occupied,
    send_list,
    send_count,
    pair_tiles,
    pair_count,
    migrate_dest,
):
    tiles = pair_tiles.shape[0]
    spans, ghosts = send_list.shape[1:]
    domains = lax.axis_size("dom")
    capacity = tiles + 2 * RADIUS * MMAX
    f32, i32 = jnp.float32, jnp.int32

    def rows_of(flat):
        return flat.reshape(tiles, TILE)

    own, ghost, dests = pl.pallas_call(
        functools.partial(frame_kernel, domains),
        out_shape=(
            jax.ShapeDtypeStruct((tiles, 8, TILE), f32),
            jax.ShapeDtypeStruct((spans, ghosts, 8, TILE), f32),
            jax.ShapeDtypeStruct((spans, 1, TILE), i32),
        ),
        in_specs=[SMEM, SMEM, VMEM, VMEM, VMEM, VMEM],
        out_specs=(VMEM, VMEM, VMEM),
        scratch_shapes=[
            pltpu.VMEM((spans, ghosts, 8, TILE), f32),
            pltpu.VMEM((1, TILE), i32),
            pltpu.SemaphoreType.DMA((spans,)),
            pltpu.SemaphoreType.DMA((spans,)),
            pltpu.SemaphoreType.DMA((spans,)),
            pltpu.SemaphoreType.DMA((spans,)),
        ],
        compiler_params=pltpu.CompilerParams(collective_id=0, has_side_effects=True),
        name="frame",
    )(
        send_list,
        send_count,
        positions,
        rows_of(density_weight),
        rows_of(occupied),
        migrate_dest.reshape(1, tiles),
    )
    ghost = ghost.reshape(spans * ghosts, 8, TILE)
    energy, slope, slope_out = pl.pallas_call(
        density_kernel,
        out_shape=(
            jax.ShapeDtypeStruct((tiles, TILE), f32),
            jax.ShapeDtypeStruct((tiles, TILE), f32),
            jax.ShapeDtypeStruct((spans, ghosts, TILE), f32),
        ),
        in_specs=[SMEM, SMEM, SMEM, VMEM, VMEM, VMEM],
        out_specs=(VMEM, VMEM, VMEM),
        scratch_shapes=[pltpu.VMEM((tiles + spans * ghosts, 4, TILE, TILE), f32)],
        compiler_params=pltpu.CompilerParams(vmem_limit_bytes=WIDE),
        name="density",
    )(pair_tiles, pair_count, send_list, own, ghost, rows_of(embed_strength))
    ghost_slope = exchange(slope_out, domains, -1, 1)
    force, outbox, stay = pl.pallas_call(
        functools.partial(force_kernel, domains),
        out_shape=(
            jax.ShapeDtypeStruct(positions.shape, f32),
            jax.ShapeDtypeStruct((spans, MMAX, 8, TILE), f32),
            jax.ShapeDtypeStruct((tiles, 8, TILE), f32),
        ),
        in_specs=[SMEM, SMEM, SMEM] + [VMEM] * 6,
        out_specs=(VMEM, VMEM, VMEM),
        scratch_shapes=[
            pltpu.VMEM((tiles + spans * ghosts, 5, TILE, TILE), f32),
            pltpu.VMEM((tiles + spans * ghosts, 8, TILE), f32),
            pltpu.SMEM((spans + 1,), i32),
        ],
        compiler_params=pltpu.CompilerParams(vmem_limit_bytes=WIDE),
        name="force",
    )(
        pair_tiles,
        pair_count,
        migrate_dest,
        own,
        ghost,
        slope,
        ghost_slope,
        positions,
        velocity,
    )
    inbox = exchange(outbox, domains, 1, 2)
    moved, moved_count = pl.pallas_call(
        settle_kernel,
        out_shape=(
            jax.ShapeDtypeStruct((7, capacity * TILE), f32),
            jax.ShapeDtypeStruct((1,), i32),
        ),
        in_specs=[SMEM, SMEM, VMEM, VMEM],
        out_specs=(VMEM, SMEM),
        name="settle",
    )(migrate_dest, dests, inbox, stay)
    return (force, energy.reshape(tiles * TILE), moved, moved_count)


def solution(mesh):
    placed = (
        P(None, "dom"),
        P(None, "dom"),
        P("dom"),
        P("dom"),
        P("dom"),
        P("dom", None, None),
        P("dom", None),
        P("dom", None),
        P("dom"),
        P("dom"),
    )
    return jax.shard_map(
        per_device,
        mesh=mesh,
        in_specs=placed,
        out_specs=(P(None, "dom"), P("dom"), P(None, "dom"), P("dom")),
        check_vma=False,
    )
```

```python
import functools

import jax
import jax.numpy as jnp
from jax import lax
from jax.experimental import pallas as pl
from jax.experimental.pallas import tpu as pltpu
from jax.sharding import PartitionSpec as P

TILE = 128
RADIUS = 4
MMAX = 4
REPULSE = 0.05
TIME_STEP = 0.05
OUTSIDE = -1000.0
MESH = pl.DeviceIdType.MESH
OFFSETS = [position - RADIUS for position in range(RADIUS)] + [
    position + 1 for position in range(RADIUS)
]
VMEM = pl.BlockSpec(memory_space=pltpu.VMEM)
SMEM = pl.BlockSpec(memory_space=pltpu.SMEM)
ANY = pl.BlockSpec(memory_space=pl.ANY)
WIDE = 60 * 1024 * 1024


def exists(device, domains):
    return jnp.logical_and(device >= 0, device < domains)


def greet(me, domains):
    barrier = pltpu.get_barrier_semaphore()
    for offset in OFFSETS:

        @pl.when(exists(me + offset, domains))
        def _():
            pl.semaphore_signal(
                barrier, inc=1, device_id=(me + offset,), device_id_type=MESH
            )

    peers = jnp.minimum(me, RADIUS) + jnp.minimum(domains - 1 - me, RADIUS)
    pl.semaphore_wait(barrier, peers)


def frame_kernel(
    domains,
    send_list,
    send_count,
    positions,
    density,
    occupied,
    dest,
    own,
    ghost,
    dests,
    outbox,
    dest_row,
    send_sem,
    recv_sem,
    dest_send,
    dest_recv,
):
    me = lax.axis_index("dom")
    tiles = own.shape[0]
    ghosts = send_list.shape[2]
    filled = occupied[...].astype(jnp.float32)
    weight = density[...] * filled
    own[...] = jnp.zeros_like(own)
    for t in range(tiles):
        here = filled[t : t + 1, :]
        half = 0.5 * here * positions[:, t * TILE : (t + 1) * TILE]
        own[t, 0:3, :] = half
        inner = 1.0 - jnp.sum(half * half, axis=0, keepdims=True)
        own[t, 3:4, :] = jnp.where(here > 0, inner, OUTSIDE)
        own[t, 4:5, :] = jnp.ones_like(here)
        own[t, 5:6, :] = weight[t : t + 1, :]
        own[t, 7:8, :] = here
    dest_row[...] = jnp.full_like(dest_row, -1)
    dest_row[:, 0:tiles] = dest[...]
    empty = empty_tile()
    for k in range(len(OFFSETS)):
        used = send_count[0, k]
        for g in range(ghosts):
            outbox[k, g] = jnp.where(g < used, own[send_list[0, k, g]], empty)
    greet(me, domains)
    for k, offset in enumerate(OFFSETS):

        @pl.when(exists(me - offset, domains))
        def _():
            pltpu.make_async_remote_copy(
                src_ref=outbox.at[k],
                dst_ref=ghost.at[k],
                send_sem=send_sem.at[k],
                recv_sem=recv_sem.at[k],
                device_id=(me - offset,),
                device_id_type=MESH,
            ).start()
            pltpu.make_async_remote_copy(
                src_ref=dest_row,
                dst_ref=dests.at[k],
                send_sem=dest_send.at[k],
                recv_sem=dest_recv.at[k],
                device_id=(me - offset,),
                device_id_type=MESH,
            ).start()

        @pl.when(jnp.logical_not(exists(me + offset, domains)))
        def _():
            for g in range(ghosts):
                ghost[k, g] = empty
            dests[k] = jnp.full(dests.shape[1:], -1, jnp.int32)

    for k, offset in enumerate(OFFSETS):

        @pl.when(exists(me - offset, domains))
        def _():
            pltpu.make_async_copy(outbox.at[k], outbox.at[k], send_sem.at[k]).wait()
            pltpu.make_async_copy(dest_row, dest_row, dest_send.at[k]).wait()

        @pl.when(exists(me + offset, domains))
        def _():
            pltpu.make_async_copy(ghost.at[k], ghost.at[k], recv_sem.at[k]).wait()
            pltpu.make_async_copy(dests.at[k], dests.at[k], dest_recv.at[k]).wait()


def exchange_kernel(domains, sign, outbox, inbox, send_sem, recv_sem):
    me = lax.axis_index("dom")
    greet(me, domains)
    for k, offset in enumerate(OFFSETS):

        @pl.when(exists(me + sign * offset, domains))
        def _():
            pltpu.make_async_remote_copy(
                src_ref=outbox.at[k],
                dst_ref=inbox.at[k],
                send_sem=send_sem.at[k],
                recv_sem=recv_sem.at[k],
                device_id=(me + sign * offset,),
                device_id_type=MESH,
            ).start()

    for k, offset in enumerate(OFFSETS):

        @pl.when(exists(me + sign * offset, domains))
        def _():
            pltpu.make_async_copy(outbox.at[k], outbox.at[k], send_sem.at[k]).wait()

        @pl.when(exists(me - sign * offset, domains))
        def _():
            pltpu.make_async_copy(inbox.at[k], inbox.at[k], recv_sem.at[k]).wait()


def exchange(blocks, domains, sign, collective_id):
    count = len(OFFSETS)
    return pl.pallas_call(
        functools.partial(exchange_kernel, domains, sign),
        out_shape=jax.ShapeDtypeStruct(blocks.shape, blocks.dtype),
        in_specs=[ANY],
        out_specs=ANY,
        scratch_shapes=[
            pltpu.SemaphoreType.DMA((count,)),
            pltpu.SemaphoreType.DMA((count,)),
        ],
        compiler_params=pltpu.CompilerParams(
            collective_id=collective_id, has_side_effects=True
        ),
        name=f"exchange_{collective_id}",
    )(blocks)


def empty_tile():
    row = lax.broadcasted_iota(jnp.int32, (8, TILE), 0)
    return jnp.where(row == 3, OUTSIDE, jnp.where(row == 4, 1.0, 0.0))


def parts(value):
    high = value.astype(jnp.bfloat16).astype(jnp.float32)
    rest = value - high
    middle = rest.astype(jnp.bfloat16).astype(jnp.float32)
    return high, middle, rest - middle


def near_side(tile):
    high, middle, low = parts(tile)
    stack = jnp.concatenate([high, middle, low, high, middle, high], axis=0)
    return stack.T.astype(jnp.bfloat16)


def own_side(tile, second):
    row = lax.broadcasted_iota(jnp.int32, (8, TILE), 0)
    outer = jnp.broadcast_to(tile[3:4] - 1.0, (8, TILE))
    first = jnp.where(row < 3, 2.0 * tile, jnp.where(row == 3, 1.0, 0.0))
    first = jnp.where(row == 4, outer, first)
    high, middle, low = parts(jnp.concatenate([first, second], axis=1))
    stack = jnp.concatenate([high, high, high, middle, middle, low], axis=0)
    return stack.astype(jnp.bfloat16)


def pair_sums(t, pair_tiles, pair_count, near, weights, even, odd, add, sums):
    used, most = pair_count[t], pair_tiles.shape[0]
    null = near.shape[0] - 1

    def tile_of(p):
        return jnp.where(p < used, pair_tiles[jnp.minimum(p, most - 1), t], null)

    def product(p):
        return jnp.dot(near[tile_of(p)], weights, preferred_element_type=jnp.float32)

    even[...] = product(0)

    def step(h, sums):
        odd[...] = product(2 * h + 1)
        sums = add(sums, even, tile_of(2 * h))
        even[...] = product(2 * h + 2)
        return add(sums, odd, tile_of(2 * h + 1))

    return lax.fori_loop(0, lax.shift_right_logical(used + 1, 1), step, sums)


def density_kernel(
    pair_tiles, pair_count, send_list, own, ghost, embed, energy, slope, outbox, near, even, odd
):
    tiles, frame_ghosts = own.shape[0], ghost.shape[0]

    def prepare(source, first):
        def step(f, carry):
            for u in range(4):
                near[first + 4 * f + u] = near_side(source[4 * f + u])
            return carry

        lax.fori_loop(0, source.shape[0] // 4, step, 0)

    prepare(own, 0)
    prepare(ghost, tiles)
    near[tiles + frame_ghosts] = near_side(empty_tile())
    row = lax.broadcasted_iota(jnp.int32, (8, TILE), 0)
    pick = jnp.where(row == 5, 1.0, 0.0)

    def tile_step(t, carry):
        mine = own[t]

        def add(sums, block, tile):
            rho, pair = sums
            for j in range(TILE // 8):
                rows = pl.ds(j * 8, 8)
                reach = jnp.maximum(block[rows, 0:TILE], 0.0)
                square = reach * reach
                rho = rho + square * reach * block[rows, TILE : 2 * TILE]
                pair = pair + square * square
            return rho, pair

        zero = jnp.zeros((8, TILE), jnp.float32)
        rho, pair = pair_sums(
            t, pair_tiles, pair_count, near, own_side(mine, pick), even, odd, add, (zero, zero)
        )
        weight, filled = mine[5:6], mine[7:8]
        rho = jnp.sum(rho, axis=0, keepdims=True) - weight
        pair = jnp.sum(pair, axis=0, keepdims=True) - filled
        root = jnp.sqrt(1.0 + rho)
        strength = embed[pl.ds(t, 1), :]
        slope[pl.ds(t, 1), :] = -0.5 * strength * filled / root
        energy[pl.ds(t, 1), :] = filled * (-strength * root + 0.5 * REPULSE * pair)
        return carry

    lax.fori_loop(0, tiles, tile_step, 0)
    for k in range(send_list.shape[1]):
        for g in range(send_list.shape[2]):
            outbox[k, g : g + 1, :] = slope[pl.ds(send_list[0, k, g], 1), :]


def force_kernel(
    domains,
    pair_tiles,
    pair_count,
    dest,
    own,
    ghost,
    slope,
    ghost_slope,
    positions,
    velocity,
    force,
    outbox,
    stay,
    near,
    even,
    odd,
    wide,
    packed,
    ranks,
):
    me = lax.axis_index("dom")
    tiles, frame_ghosts = own.shape[0], ghost.shape[0]
    spans = len(OFFSETS)
    each = frame_ghosts // spans
    packed[0:tiles] = own[...]
    packed[tiles:] = ghost[...]
    for t in range(tiles):
        packed[t, 6:7, :] = 3.0 * slope[t : t + 1, :]
    for k, offset in enumerate(OFFSETS):
        real = exists(me + offset, domains)
        for g in range(each):
            packed[tiles + k * each + g, 6:7, :] = jnp.where(
                real, 3.0 * ghost_slope[k, g : g + 1, :], 0.0
            )
    group = TILE // 8

    def prepare(b, carry):
        block = packed[pl.ds(b * group, group)].reshape(TILE, TILE).T
        for f in range(group):
            near[b * group + f] = near_side(packed[b * group + f])
            for c in range(3):
                lane = f * 8 + c
                wide[b * group + f, c] = jnp.broadcast_to(
                    block[:, lane : lane + 1], (TILE, TILE)
                )
        return carry

    lax.fori_loop(0, (tiles + frame_ghosts) // group, prepare, 0)
    near[tiles + frame_ghosts] = near_side(empty_tile())
    wide[tiles + frame_ghosts] = jnp.zeros(wide.shape[1:], jnp.float32)
    for k in range(spans + 1):
        ranks[k] = 0
    row = lax.broadcasted_iota(jnp.int32, (8, TILE), 0)

    def tile_step(t, carry):
        mine = packed[t]
        weight = jnp.broadcast_to(mine[5:6], (8, TILE))
        tilt = jnp.broadcast_to(mine[6:7], (8, TILE))
        mixing = jnp.where(row == 5, tilt, jnp.where(row == 6, weight, 0.0))

        def add(sums, block, tile):
            total, fx, fy, fz = sums
            for j in range(TILE // 8):
                rows = pl.ds(j * 8, 8)
                reach = jnp.maximum(block[rows, 0:TILE], 0.0)
                mixed = block[rows, TILE : 2 * TILE] + (4.0 * REPULSE) * reach
                coef = reach * reach * mixed
                total = total + coef
                fx = fx + coef * wide[tile, 0, rows]
                fy = fy + coef * wide[tile, 1, rows]
                fz = fz + coef * wide[tile, 2, rows]
            return total, fx, fy, fz

        zero = jnp.zeros((8, TILE), jnp.float32)
        sums = pair_sums(
            t, pair_tiles, pair_count, near, own_side(mine, mixing), even, odd, add, (zero,) * 4
        )
        total, *pulls = [jnp.sum(s, axis=0, keepdims=True) for s in sums]
        filled = mine[7:8]
        columns = pl.ds(pl.multiple_of(t * TILE, TILE), TILE)
        pull = filled * (mine[0:3] * total - jnp.concatenate(pulls, axis=0))
        force[:, columns] = pull
        new_vel = velocity[:, columns] + TIME_STEP * pull
        new_pos = positions[:, columns] + TIME_STEP * new_vel
        tile = jnp.concatenate([new_pos, new_vel, filled, jnp.zeros_like(filled)], axis=0)
        relative = dest[t] - me
        place = jnp.where(relative < 0, relative + RADIUS, relative + RADIUS - 1)
        place = jnp.where(relative == 0, spans, place)
        rank = ranks[place]
        ranks[place] = rank + 1

        @pl.when(relative == 0)
        def _():
            stay[rank] = tile

        @pl.when(relative != 0)
        def _():
            outbox[place, rank] = tile

        return carry

    lax.fori_loop(0, tiles, tile_step, 0)


def settle_kernel(dest, dests, inbox, stay, moved, count):
    me = lax.axis_index("dom")
    tiles, slots = dest.shape[0], moved.shape[1] // TILE
    rows = moved.shape[0]
    spans = len(OFFSETS)

    def put(e, tile, atoms):
        moved[:, pl.ds(pl.multiple_of(e * TILE, TILE), TILE)] = tile[0:rows]
        return atoms + tile

    def hits(value_of):
        total = jnp.int32(0)
        for i in range(tiles):
            total = total + (value_of(i) == me).astype(jnp.int32)
        return total

    slot = jnp.int32(0)
    atoms = jnp.zeros((8, TILE), jnp.float32)

    for k in range(spans):
        if k == RADIUS:
            here = hits(lambda i: dest[i])
            atoms = lax.fori_loop(
                0, here, lambda r, a, s=slot: put(s + r, stay[r], a), atoms
            )
            slot = slot + here
        here = hits(lambda i: dests[k, 0, i])
        atoms = lax.fori_loop(
            0, here, lambda r, a, s=slot: put(s + r, inbox[spans - 1 - k, r], a), atoms
        )
        slot = slot + here

    def clear(e, carry):
        moved[:, pl.ds(pl.multiple_of(e * TILE, TILE), TILE)] = jnp.zeros(
            (rows, TILE), jnp.float32
        )
        return carry

    lax.fori_loop(slot, slots, clear, 0)
    count[0] = jnp.sum(atoms[6:7]).astype(jnp.int32)


def per_device(
    positions,
    velocity,
    density_weight,
    embed_strength,
    occupied,
    send_list,
    send_count,
    pair_tiles,
    pair_count,
    migrate_dest,
):
    tiles = pair_tiles.shape[0]
    spans, ghosts = send_list.shape[1:]
    domains = lax.axis_size("dom")
    capacity = tiles + 2 * RADIUS * MMAX
    f32, i32 = jnp.float32, jnp.int32

    def rows_of(flat):
        return flat.reshape(tiles, TILE)

    own, ghost, dests = pl.pallas_call(
        functools.partial(frame_kernel, domains),
        out_shape=(
            jax.ShapeDtypeStruct((tiles, 8, TILE), f32),
            jax.ShapeDtypeStruct((spans, ghosts, 8, TILE), f32),
            jax.ShapeDtypeStruct((spans, 1, TILE), i32),
        ),
        in_specs=[SMEM, SMEM, VMEM, VMEM, VMEM, VMEM],
        out_specs=(VMEM, VMEM, VMEM),
        scratch_shapes=[
            pltpu.VMEM((spans, ghosts, 8, TILE), f32),
            pltpu.VMEM((1, TILE), i32),
            pltpu.SemaphoreType.DMA((spans,)),
            pltpu.SemaphoreType.DMA((spans,)),
            pltpu.SemaphoreType.DMA((spans,)),
            pltpu.SemaphoreType.DMA((spans,)),
        ],
        compiler_params=pltpu.CompilerParams(collective_id=0, has_side_effects=True),
        name="frame",
    )(
        send_list,
        send_count,
        positions,
        rows_of(density_weight),
        rows_of(occupied),
        migrate_dest.reshape(1, tiles),
    )
    ghost = ghost.reshape(spans * ghosts, 8, TILE)
    energy, slope, slope_out = pl.pallas_call(
        density_kernel,
        out_shape=(
            jax.ShapeDtypeStruct((tiles, TILE), f32),
            jax.ShapeDtypeStruct((tiles, TILE), f32),
            jax.ShapeDtypeStruct((spans, ghosts, TILE), f32),
        ),
        in_specs=[SMEM, SMEM, SMEM, VMEM, VMEM, VMEM],
        out_specs=(VMEM, VMEM, VMEM),
        scratch_shapes=[
            pltpu.VMEM((tiles + spans * ghosts + 1, TILE, 48), jnp.bfloat16),
            pltpu.VMEM((TILE, 2 * TILE), f32),
            pltpu.VMEM((TILE, 2 * TILE), f32),
        ],
        compiler_params=pltpu.CompilerParams(vmem_limit_bytes=WIDE),
        name="density",
    )(pair_tiles.T, pair_count, send_list, own, ghost, rows_of(embed_strength))
    ghost_slope = exchange(slope_out, domains, -1, 1)
    force, outbox, stay = pl.pallas_call(
        functools.partial(force_kernel, domains),
        out_shape=(
            jax.ShapeDtypeStruct(positions.shape, f32),
            jax.ShapeDtypeStruct((spans, MMAX, 8, TILE), f32),
            jax.ShapeDtypeStruct((tiles, 8, TILE), f32),
        ),
        in_specs=[SMEM, SMEM, SMEM] + [VMEM] * 6,
        out_specs=(VMEM, VMEM, VMEM),
        scratch_shapes=[
            pltpu.VMEM((tiles + spans * ghosts + 1, TILE, 48), jnp.bfloat16),
            pltpu.VMEM((TILE, 2 * TILE), f32),
            pltpu.VMEM((TILE, 2 * TILE), f32),
            pltpu.VMEM((tiles + spans * ghosts + 1, 3, TILE, TILE), f32),
            pltpu.VMEM((tiles + spans * ghosts, 8, TILE), f32),
            pltpu.SMEM((spans + 1,), i32),
        ],
        compiler_params=pltpu.CompilerParams(vmem_limit_bytes=WIDE),
        name="force",
    )(
        pair_tiles.T,
        pair_count,
        migrate_dest,
        own,
        ghost,
        slope,
        ghost_slope,
        positions,
        velocity,
    )
    inbox = exchange(outbox, domains, 1, 2)
    moved, moved_count = pl.pallas_call(
        settle_kernel,
        out_shape=(
            jax.ShapeDtypeStruct((7, capacity * TILE), f32),
            jax.ShapeDtypeStruct((1,), i32),
        ),
        in_specs=[SMEM, SMEM, VMEM, VMEM],
        out_specs=(VMEM, SMEM),
        name="settle",
    )(migrate_dest, dests, inbox, stay)
    return (force, energy.reshape(tiles * TILE), moved, moved_count)


def solution(mesh):
    placed = (
        P(None, "dom"),
        P(None, "dom"),
        P("dom"),
        P("dom"),
        P("dom"),
        P("dom", None, None),
        P("dom", None),
        P("dom", None),
        P("dom"),
        P("dom"),
    )
    return jax.shard_map(
        per_device,
        mesh=mesh,
        in_specs=placed,
        out_specs=(P(None, "dom"), P("dom"), P(None, "dom"), P("dom")),
        check_vma=False,
    )
```

```python
import functools

import jax
import jax.numpy as jnp
from jax import lax
from jax.experimental import pallas as pl
from jax.experimental.pallas import tpu as pltpu
from jax.sharding import PartitionSpec as P

TILE = 128
RADIUS = 4
MMAX = 4
REPULSE = 0.05
TIME_STEP = 0.05
AWAY = 1e3
OUTSIDE = -1e9
MESH = pl.DeviceIdType.MESH
OFFSETS = [position - RADIUS for position in range(RADIUS)] + [
    position + 1 for position in range(RADIUS)
]
VMEM = pl.BlockSpec(memory_space=pltpu.VMEM)
SMEM = pl.BlockSpec(memory_space=pltpu.SMEM)
ANY = pl.BlockSpec(memory_space=pl.ANY)
WIDE = 60 * 1024 * 1024


def exists(device, domains):
    return jnp.logical_and(device >= 0, device < domains)


def greet(me, domains):
    barrier = pltpu.get_barrier_semaphore()
    for offset in OFFSETS:

        @pl.when(exists(me + offset, domains))
        def _():
            pl.semaphore_signal(
                barrier, inc=1, device_id=(me + offset,), device_id_type=MESH
            )

    peers = jnp.minimum(me, RADIUS) + jnp.minimum(domains - 1 - me, RADIUS)
    pl.semaphore_wait(barrier, peers)


def frame_kernel(
    domains,
    send_list,
    send_count,
    positions,
    density,
    occupied,
    dest,
    own,
    ghost,
    dests,
    outbox,
    dest_row,
    send_sem,
    recv_sem,
    dest_send,
    dest_recv,
):
    me = lax.axis_index("dom")
    tiles = own.shape[0]
    ghosts = send_list.shape[2]
    filled = occupied[...].astype(jnp.float32)
    weight = density[...] * filled
    own[...] = jnp.zeros_like(own)
    for t in range(tiles):
        here = filled[t : t + 1, :]
        half = 0.5 * positions[:, t * TILE : (t + 1) * TILE]
        own[t, 0:3, :] = jnp.where(here > 0, half, AWAY)
        inner = 1.0 - jnp.sum(half * half, axis=0, keepdims=True)
        own[t, 3:4, :] = jnp.where(here > 0, inner, OUTSIDE)
        own[t, 5:6, :] = weight[t : t + 1, :]
        own[t, 7:8, :] = here
    dest_row[...] = jnp.full_like(dest_row, -1)
    dest_row[:, 0:tiles] = dest[...]
    empty = empty_tile()
    for k in range(len(OFFSETS)):
        used = send_count[0, k]
        for g in range(ghosts):
            outbox[k, g] = jnp.where(g < used, own[send_list[0, k, g]], empty)
    greet(me, domains)
    for k, offset in enumerate(OFFSETS):

        @pl.when(exists(me - offset, domains))
        def _():
            pltpu.make_async_remote_copy(
                src_ref=outbox.at[k],
                dst_ref=ghost.at[k],
                send_sem=send_sem.at[k],
                recv_sem=recv_sem.at[k],
                device_id=(me - offset,),
                device_id_type=MESH,
            ).start()
            pltpu.make_async_remote_copy(
                src_ref=dest_row,
                dst_ref=dests.at[k],
                send_sem=dest_send.at[k],
                recv_sem=dest_recv.at[k],
                device_id=(me - offset,),
                device_id_type=MESH,
            ).start()

        @pl.when(jnp.logical_not(exists(me + offset, domains)))
        def _():
            for g in range(ghosts):
                ghost[k, g] = empty
            dests[k] = jnp.full(dests.shape[1:], -1, jnp.int32)

    for k, offset in enumerate(OFFSETS):

        @pl.when(exists(me - offset, domains))
        def _():
            pltpu.make_async_copy(outbox.at[k], outbox.at[k], send_sem.at[k]).wait()
            pltpu.make_async_copy(dest_row, dest_row, dest_send.at[k]).wait()

        @pl.when(exists(me + offset, domains))
        def _():
            pltpu.make_async_copy(ghost.at[k], ghost.at[k], recv_sem.at[k]).wait()
            pltpu.make_async_copy(dests.at[k], dests.at[k], dest_recv.at[k]).wait()


def exchange_kernel(domains, sign, outbox, inbox, send_sem, recv_sem):
    me = lax.axis_index("dom")
    greet(me, domains)
    for k, offset in enumerate(OFFSETS):

        @pl.when(exists(me + sign * offset, domains))
        def _():
            pltpu.make_async_remote_copy(
                src_ref=outbox.at[k],
                dst_ref=inbox.at[k],
                send_sem=send_sem.at[k],
                recv_sem=recv_sem.at[k],
                device_id=(me + sign * offset,),
                device_id_type=MESH,
            ).start()

    for k, offset in enumerate(OFFSETS):

        @pl.when(exists(me + sign * offset, domains))
        def _():
            pltpu.make_async_copy(outbox.at[k], outbox.at[k], send_sem.at[k]).wait()

        @pl.when(exists(me - sign * offset, domains))
        def _():
            pltpu.make_async_copy(inbox.at[k], inbox.at[k], recv_sem.at[k]).wait()


def exchange(blocks, domains, sign, collective_id):
    count = len(OFFSETS)
    return pl.pallas_call(
        functools.partial(exchange_kernel, domains, sign),
        out_shape=jax.ShapeDtypeStruct(blocks.shape, blocks.dtype),
        in_specs=[VMEM],
        out_specs=VMEM,
        scratch_shapes=[
            pltpu.SemaphoreType.DMA((count,)),
            pltpu.SemaphoreType.DMA((count,)),
        ],
        compiler_params=pltpu.CompilerParams(
            collective_id=collective_id, has_side_effects=True
        ),
        name=f"exchange_{collective_id}",
    )(blocks)


def empty_tile():
    row = lax.broadcasted_iota(jnp.int32, (8, TILE), 0)
    return jnp.where(row < 3, AWAY, jnp.where(row == 3, OUTSIDE, 0.0))


def spread(source, first, wide, rows):
    group = TILE // 8

    def step(b, carry):
        block = source[pl.ds(b * group, group)].reshape(TILE, TILE).T
        for f in range(group):
            for n, c in enumerate(rows):
                lane = f * 8 + c
                wide[first + b * group + f, n] = jnp.broadcast_to(
                    block[:, lane : lane + 1], (TILE, TILE)
                )
        return carry

    lax.fori_loop(0, source.shape[0] // group, step, 0)


def spread_empty(wide, rows):
    for n, c in enumerate(rows):
        value = AWAY if c < 3 else OUTSIDE if c == 3 else 0.0
        wide[wide.shape[0] - 1, n] = jnp.full((TILE, TILE), value, jnp.float32)


def pair_sums(t, pair_tiles, pair_count, null, add, sums):
    used, most = pair_count[t], pair_tiles.shape[0]

    def step(h, sums):
        later = 2 * h + 1
        tile = jnp.where(later < used, pair_tiles[jnp.minimum(later, most - 1), t], null)
        return add(add(sums, pair_tiles[2 * h, t]), tile)

    return lax.fori_loop(0, lax.shift_right_logical(used + 1, 1), step, sums)


def density_kernel(
    pair_tiles, pair_count, send_list, own, ghost, embed, energy, slope, outbox, wide
):
    tiles = own.shape[0]
    rows_used = (0, 1, 2, 3, 5)
    spread(own, 0, wide, rows_used)
    spread(ghost, tiles, wide, rows_used)
    spread_empty(wide, rows_used)

    def tile_step(t, carry):
        mine = own[t]
        x, y, z = [jnp.broadcast_to(2.0 * mine[c : c + 1], (8, TILE)) for c in range(3)]
        norm = jnp.broadcast_to(1.0 - mine[3:4], (8, TILE))

        def add(sums, near):
            rho, pair = sums
            for j in range(TILE // 8):
                rows = pl.ds(j * 8, 8)
                inner = (x * wide[near, 0, rows] + y * wide[near, 1, rows]) + (
                    z * wide[near, 2, rows] + wide[near, 3, rows]
                )
                reach = jnp.maximum(inner - norm, 0.0)
                square = reach * reach
                rho = rho + square * reach * wide[near, 4, rows]
                pair = pair + square * square
            return rho, pair

        zero = jnp.zeros((8, TILE), jnp.float32)
        rho, pair = pair_sums(
            t, pair_tiles, pair_count, wide.shape[0] - 1, add, (zero, zero)
        )
        weight, filled = mine[5:6], mine[7:8]
        rho = jnp.sum(rho, axis=0, keepdims=True) - weight
        pair = jnp.sum(pair, axis=0, keepdims=True) - filled
        root = jnp.sqrt(1.0 + rho)
        strength = embed[pl.ds(t, 1), :]
        slope[pl.ds(t, 1), :] = -0.5 * strength * filled / root
        energy[pl.ds(t, 1), :] = filled * (-strength * root + 0.5 * REPULSE * pair)
        return carry

    lax.fori_loop(0, tiles, tile_step, 0)
    for k in range(send_list.shape[1]):
        for g in range(send_list.shape[2]):
            outbox[k, g : g + 1, :] = slope[pl.ds(send_list[0, k, g], 1), :]


def force_kernel(
    domains,
    pair_tiles,
    pair_count,
    dest,
    own,
    ghost,
    slope,
    ghost_slope,
    positions,
    velocity,
    force,
    outbox,
    stay,
    wide,
    packed,
    ranks,
):
    me = lax.axis_index("dom")
    tiles, frame_ghosts = own.shape[0], ghost.shape[0]
    spans = len(OFFSETS)
    each = frame_ghosts // spans
    packed[0:tiles] = own[...]
    packed[tiles:] = ghost[...]
    for t in range(tiles):
        packed[t, 6:7, :] = (0.75 / REPULSE) * slope[t : t + 1, :]
    for k, offset in enumerate(OFFSETS):
        real = exists(me + offset, domains)
        for g in range(each):
            packed[tiles + k * each + g, 6:7, :] = jnp.where(
                real, (0.75 / REPULSE) * ghost_slope[k, g : g + 1, :], 0.0
            )
    rows_used = (0, 1, 2, 5, 6)
    spread(packed, 0, wide, rows_used)
    spread_empty(wide, rows_used)
    for k in range(spans + 1):
        ranks[k] = 0

    def tile_step(t, carry):
        mine = packed[t]
        x, y, z, weight, tilt = [
            jnp.broadcast_to(mine[c : c + 1], (8, TILE)) for c in rows_used
        ]

        def add(sums, near):
            fx, fy, fz = sums
            for j in range(TILE // 8):
                rows = pl.ds(j * 8, 8)
                dx = x - wide[near, 0, rows]
                dy = y - wide[near, 1, rows]
                dz = z - wide[near, 2, rows]
                reach = jnp.maximum(1.0 - (dx * dx + dy * dy + dz * dz), 0.0)
                mixed = tilt * wide[near, 3, rows] + weight * wide[near, 4, rows]
                coef = reach * reach * (mixed + reach)
                fx = fx + coef * dx
                fy = fy + coef * dy
                fz = fz + coef * dz
            return fx, fy, fz

        zero = jnp.zeros((8, TILE), jnp.float32)
        sums = pair_sums(
            t, pair_tiles, pair_count, wide.shape[0] - 1, add, (zero, zero, zero)
        )
        filled = mine[7:8]
        columns = pl.ds(pl.multiple_of(t * TILE, TILE), TILE)
        pull = (4.0 * REPULSE) * filled * jnp.concatenate(
            [jnp.sum(s, axis=0, keepdims=True) for s in sums], axis=0
        )
        force[:, columns] = pull
        new_vel = velocity[:, columns] + TIME_STEP * pull
        new_pos = positions[:, columns] + TIME_STEP * new_vel
        tile = jnp.concatenate([new_pos, new_vel, filled, jnp.zeros_like(filled)], axis=0)
        relative = dest[t] - me
        place = jnp.where(relative < 0, relative + RADIUS, relative + RADIUS - 1)
        place = jnp.where(relative == 0, spans, place)
        rank = ranks[place]
        ranks[place] = rank + 1

        @pl.when(relative == 0)
        def _():
            stay[rank] = tile

        @pl.when(relative != 0)
        def _():
            outbox[place, rank] = tile

        return carry

    lax.fori_loop(0, tiles, tile_step, 0)


def settle_kernel(dest, dests, inbox, stay, moved, count):
    me = lax.axis_index("dom")
    tiles, slots = dest.shape[0], moved.shape[1] // TILE
    rows = moved.shape[0]
    spans = len(OFFSETS)

    def put(e, tile, atoms):
        moved[:, pl.ds(pl.multiple_of(e * TILE, TILE), TILE)] = tile[0:rows]
        return atoms + tile

    def hits(value_of):
        total = jnp.int32(0)
        for i in range(tiles):
            total = total + (value_of(i) == me).astype(jnp.int32)
        return total

    slot = jnp.int32(0)
    atoms = jnp.zeros((8, TILE), jnp.float32)

    for k in range(spans):
        if k == RADIUS:
            here = hits(lambda i: dest[i])
            atoms = lax.fori_loop(
                0, here, lambda r, a, s=slot: put(s + r, stay[r], a), atoms
            )
            slot = slot + here
        here = hits(lambda i: dests[k, 0, i])
        atoms = lax.fori_loop(
            0, here, lambda r, a, s=slot: put(s + r, inbox[spans - 1 - k, r], a), atoms
        )
        slot = slot + here

    def clear(e, carry):
        moved[:, pl.ds(pl.multiple_of(e * TILE, TILE), TILE)] = jnp.zeros(
            (rows, TILE), jnp.float32
        )
        return carry

    lax.fori_loop(slot, slots, clear, 0)
    count[0] = jnp.sum(atoms[6:7]).astype(jnp.int32)


def per_device(
    positions,
    velocity,
    density_weight,
    embed_strength,
    occupied,
    send_list,
    send_count,
    pair_tiles,
    pair_count,
    migrate_dest,
):
    tiles = pair_tiles.shape[0]
    spans, ghosts = send_list.shape[1:]
    domains = lax.axis_size("dom")
    capacity = tiles + 2 * RADIUS * MMAX
    f32, i32 = jnp.float32, jnp.int32

    def rows_of(flat):
        return flat.reshape(tiles, TILE)

    own, ghost, dests = pl.pallas_call(
        functools.partial(frame_kernel, domains),
        out_shape=(
            jax.ShapeDtypeStruct((tiles, 8, TILE), f32),
            jax.ShapeDtypeStruct((spans, ghosts, 8, TILE), f32),
            jax.ShapeDtypeStruct((spans, 1, TILE), i32),
        ),
        in_specs=[SMEM, SMEM, VMEM, VMEM, VMEM, VMEM],
        out_specs=(VMEM, VMEM, VMEM),
        scratch_shapes=[
            pltpu.VMEM((spans, ghosts, 8, TILE), f32),
            pltpu.VMEM((1, TILE), i32),
            pltpu.SemaphoreType.DMA((spans,)),
            pltpu.SemaphoreType.DMA((spans,)),
            pltpu.SemaphoreType.DMA((spans,)),
            pltpu.SemaphoreType.DMA((spans,)),
        ],
        compiler_params=pltpu.CompilerParams(collective_id=0, has_side_effects=True),
        name="frame",
    )(
        send_list,
        send_count,
        positions,
        rows_of(density_weight),
        rows_of(occupied),
        migrate_dest.reshape(1, tiles),
    )
    ghost = ghost.reshape(spans * ghosts, 8, TILE)
    energy, slope, slope_out = pl.pallas_call(
        density_kernel,
        out_shape=(
            jax.ShapeDtypeStruct((tiles, TILE), f32),
            jax.ShapeDtypeStruct((tiles, TILE), f32),
            jax.ShapeDtypeStruct((spans, ghosts, TILE), f32),
        ),
        in_specs=[SMEM, SMEM, SMEM, VMEM, VMEM, VMEM],
        out_specs=(VMEM, VMEM, VMEM),
        scratch_shapes=[
            pltpu.VMEM((tiles + spans * ghosts + 1, 5, TILE, TILE), f32),
        ],
        compiler_params=pltpu.CompilerParams(vmem_limit_bytes=WIDE),
        name="density",
    )(pair_tiles.T, pair_count, send_list, own, ghost, rows_of(embed_strength))
    ghost_slope = exchange(slope_out, domains, -1, 1)
    force, outbox, stay = pl.pallas_call(
        functools.partial(force_kernel, domains),
        out_shape=(
            jax.ShapeDtypeStruct(positions.shape, f32),
            jax.ShapeDtypeStruct((spans, MMAX, 8, TILE), f32),
            jax.ShapeDtypeStruct((tiles, 8, TILE), f32),
        ),
        in_specs=[SMEM, SMEM, SMEM] + [VMEM] * 6,
        out_specs=(VMEM, VMEM, VMEM),
        scratch_shapes=[
            pltpu.VMEM((tiles + spans * ghosts + 1, 5, TILE, TILE), f32),
            pltpu.VMEM((tiles + spans * ghosts, 8, TILE), f32),
            pltpu.SMEM((spans + 1,), i32),
        ],
        compiler_params=pltpu.CompilerParams(vmem_limit_bytes=WIDE),
        name="force",
    )(
        pair_tiles.T,
        pair_count,
        migrate_dest,
        own,
        ghost,
        slope,
        ghost_slope,
        positions,
        velocity,
    )
    inbox = exchange(outbox, domains, 1, 2)
    moved, moved_count = pl.pallas_call(
        settle_kernel,
        out_shape=(
            jax.ShapeDtypeStruct((7, capacity * TILE), f32),
            jax.ShapeDtypeStruct((1,), i32),
        ),
        in_specs=[SMEM, SMEM, VMEM, VMEM],
        out_specs=(VMEM, SMEM),
        name="settle",
    )(migrate_dest, dests, inbox, stay)
    return (force, energy.reshape(tiles * TILE), moved, moved_count)


def solution(mesh):
    placed = (
        P(None, "dom"),
        P(None, "dom"),
        P("dom"),
        P("dom"),
        P("dom"),
        P("dom", None, None),
        P("dom", None),
        P("dom", None),
        P("dom"),
        P("dom"),
    )
    return jax.shard_map(
        per_device,
        mesh=mesh,
        in_specs=placed,
        out_specs=(P(None, "dom"), P("dom"), P(None, "dom"), P("dom")),
        check_vma=False,
    )
```
